32 devices in a mesh: rows: 8 (over z, y), cols: 4 (over x, core).
Axes of the slice: x: 2, y: 2, z: 4, core: 2. Of those that a mesh axis runs over, the one named last changes fastest.
Arguments:
- start_panel: float32 [64, 16384], P(None, ('rows', 'cols')), may hold values from -6 to 6
- tile_values: float32 [128, 16, 128, 128], P('rows', 'cols')
- tile_column: int32 [128, 16], P('rows', 'cols'), may hold values from 0 to 127, as said below
- tile_count: int32 [128], P('rows'), may hold values from 8 to 16, as said below
Outputs:
- basis: float32 [64, 16384], P(None, ('rows', 'cols'))
The draws below stay inside these ranges and needn't reach their ends.
Inputs may be any that keep to these rules, and one draw needn't show every extreme that they name: `tile_count`: every row block has between half of its slots and all 16 slots live; some row block has all 16 live. `tile_column`: in row block i the entries are distinct column blocks, each within 16 blocks of i, and the first is i itself; slots at or beyond tile_count[i] hold such entries too but are not used.
All inputs are finite; a program needn't handle non-finite values.
Results may differ from the reference program's by a relative error of at most 0.0003.
Values sent between devices are 32-bit elements; how exact they have to be, the bound alone decides.
A program may use at most 64 MiB of HBM per device.

```python
import math
import jax
import jax.numpy as jnp
from jax import lax

TILE = 128
PANEL = 64
RB_DEV = 16
ITERS = 3
NB = 128
SLOTS = 16
STATES = 16384


def draw_tile_values(key, part):
    noise_key = jax.random.fold_in(key, 11)
    level_key = jax.random.fold_in(key, 12)
    spread = 0.6 / math.sqrt(TILE * SLOTS * 0.75)
    noise = jax.random.normal(noise_key, (NB, SLOTS, TILE, TILE), jnp.float32) * spread
    levels = jnp.exp(jax.random.uniform(level_key, (NB, TILE), jnp.float32, math.log(0.6), math.log(1.2)))
    ramp = jnp.sqrt(1.0 + jnp.arange(NB, dtype=jnp.float32) / NB)
    levels = levels * ramp[:, None]
    identity = jnp.eye(TILE, dtype=jnp.float32)
    diagonal_tiles = levels[:, :, None] * identity[None, :, :]
    return noise.at[:, 0].add(diagonal_tiles)


def draw_tile_column(key, part):
    offsets = jnp.concatenate([jnp.arange(-RB_DEV, 0, dtype=jnp.int32), jnp.arange(1, RB_DEV + 1, dtype=jnp.int32)])
    row_ids = jnp.arange(NB, dtype=jnp.int32)[:, None]
    candidates = row_ids + offsets[None, :]
    inside = ((candidates >= 0) & (candidates < NB)).astype(jnp.int32)
    random_part = jax.random.randint(jax.random.fold_in(key, 21), (NB, 2 * RB_DEV), 0, 8192)
    scores = inside * 16777216 + random_part * 1024 + jnp.arange(2 * RB_DEV, dtype=jnp.int32)[None, :]
    top_scores, chosen = lax.top_k(scores, SLOTS - 1)
    picked = jnp.take_along_axis(candidates, chosen, axis=1)
    return jnp.concatenate([row_ids, picked], axis=1).astype(jnp.int32)


def draw_tile_count(key, part):
    counts = jax.random.randint(jax.random.fold_in(key, 31), (NB,), SLOTS // 2, SLOTS + 1)
    fullest = jax.random.randint(jax.random.fold_in(key, 32), (), 0, NB)
    return jnp.where(jnp.arange(NB, dtype=jnp.int32) == fullest, SLOTS, counts).astype(jnp.int32)


def block_levels(key, extent, cuts, low, largest):
    loudness, own = 1.0, jax.random.fold_in(key, 6)
    for position, shards_of in cuts:
        draws = jnp.exp(jax.random.uniform(jax.random.fold_in(own, position), (shards_of,), jnp.float32, low / len(cuts), largest / len(cuts)))
        loudness = loudness * jnp.repeat(draws, extent[position] // shards_of).reshape([-1 if axis == position else 1 for axis in range(len(extent))])
    return loudness


def scatter_about(key, shape, deviation, limit, pieces=(), kind=jnp.bfloat16):
    values = deviation * jax.random.normal(key, shape, jnp.float32)
    if pieces:
        values = values * block_levels(key, shape, pieces, -0.22, 0.18)
    return jnp.clip(values, -limit, limit).astype(kind)


def setup_inputs(seed: int = 0) -> dict:
    arg_keys = jax.random.split(jax.random.key(seed), 5)
    start_panel = scatter_about(arg_keys[0], (PANEL, STATES), 1.0, 6.0, ((1, 32),), jnp.float32)
    tile_values = draw_tile_values(jax.random.fold_in(arg_keys[4], 71), 0)
    tile_column = draw_tile_column(jax.random.fold_in(arg_keys[4], 71), 0)
    tile_count = draw_tile_count(jax.random.fold_in(arg_keys[4], 71), 0)
    return dict(start_panel=start_panel, tile_values=tile_values, tile_column=tile_column, tile_count=tile_count)


def apply_matrix(panel, tile_values, tile_column, tile_count):
    blocks = panel.reshape(PANEL, NB, TILE)
    slot_ids = jnp.arange(SLOTS, dtype=jnp.int32)

    def one_block(item):
        tiles, columns, count = item
        picked = jnp.take(blocks, columns, axis=1)
        alive_mask = slot_ids < count
        picked = jnp.where(alive_mask[None, :, None], picked, jnp.zeros((), picked.dtype))
        return jnp.einsum('dsk,snk->dn', picked, tiles, precision=lax.Precision.HIGHEST)
    result = lax.map(one_block, (tile_values, tile_column, tile_count))
    return jnp.transpose(result, (1, 0, 2)).reshape(PANEL, STATES)

def orthonormal(second):
    gram_matrix = jnp.dot(second.astype(jnp.float32), second.T.astype(jnp.float32), precision=lax.Precision.HIGHEST, preferred_element_type=jnp.float32)
    lower_factor = jnp.linalg.cholesky(gram_matrix)
    return lax.linalg.triangular_solve(lower_factor, second, left_side=True, lower=True)

def reference(start_panel, tile_values, tile_column, tile_count):
    panel = start_panel
    for sweep_index in range(ITERS):
        first = apply_matrix(panel, tile_values, tile_column, tile_count)
        second = apply_matrix(first, tile_values, tile_column, tile_count)
        panel = orthonormal(second)
    return panel * jnp.sqrt(jnp.float32(STATES))
```

```python
import functools
import math

import jax
import jax.numpy as jnp
from jax import lax
from jax.experimental import pallas as pl
from jax.experimental.pallas import tpu as pltpu
from jax.sharding import PartitionSpec as P

ITERS = 3
HIGHEST = lax.Precision.HIGHEST
F32 = jnp.float32
BF16 = jnp.bfloat16

GATHER, LOW, HIGH, LOW_X, HIGH_X, REDUCE, SPREAD, PAIR = range(8)
KINDS = 8


def inverse_factor(gram):
    size = gram.shape[0]
    rows = lax.broadcasted_iota(jnp.int32, (size, size), 0)
    lanes = lax.broadcasted_iota(jnp.int32, (size, size), 1)
    both = jnp.concatenate([gram, jnp.where(rows == lanes, 1.0, 0.0).astype(F32)], axis=1)
    row_ids = lax.broadcasted_iota(jnp.int32, (size, 1), 0)
    scale = jnp.ones((size, 1), F32)
    for j in range(size):
        column = both[:, j : j + 1]
        row = both[j : j + 1, :]
        pivot = both[j : j + 1, j : j + 1]
        factor = jnp.where(row_ids > j, column / pivot, 0.0)
        scale = jnp.where(row_ids == j, lax.rsqrt(pivot), scale)
        both = both - factor * row
    return both[:, size:] * scale


def kernel(
    n_rows, start_ref, tiles_ref, slots_ref, out_ref,
    ext, planes, part, reduced, summed, share, pair, own_tiles, mate_tiles, t_hi, t_lo,
    mate_slots, own_index, mate_index, weight, gram_send, gram_recv,
    send_sem, recv_sem, gram_send_sem, gram_recv_sem, tile_sem, tile_send_sem, tile_recv_sem,
    slot_sem,
):
    r = lax.axis_index("rows")
    c = lax.axis_index("cols")
    half = c // 2
    mode = c % 2
    modes = ext.shape[2]
    owned = part.shape[0]
    hb = owned // 2
    qb = owned // 4
    slot_dev = own_tiles.shape[1]
    width = part.shape[2]
    other_half = c + 2 - 4 * half
    mate = c + 1 - 2 * mode
    row_rounds = int(math.log2(n_rows))

    def xor_rows(b):
        step = 1 << b
        bit = (r // step) % 2
        return r + step - 2 * step * bit

    gram_partners = [{"cols": mate}, {"cols": other_half}]
    gram_partners += [{"rows": xor_rows(b)} for b in range(row_rounds)]

    barrier = pltpu.get_barrier_semaphore()
    for partner in gram_partners:
        pl.semaphore_signal(barrier, inc=1, device_id=partner, device_id_type=pl.DeviceIdType.MESH)
    has_low = r > 0
    has_high = r < n_rows - 1

    @pl.when(has_low)
    def _():
        pl.semaphore_signal(barrier, inc=1, device_id={"rows": r - 1}, device_id_type=pl.DeviceIdType.MESH)

    @pl.when(has_high)
    def _():
        pl.semaphore_signal(barrier, inc=1, device_id={"rows": r + 1}, device_id_type=pl.DeviceIdType.MESH)

    edges = jnp.where(r == 0, 1, 0) + jnp.where(r == n_rows - 1, 1, 0)
    pl.semaphore_wait(barrier, len(gram_partners) + 2 - edges)

    def remote(src, dst, t, kind, device):
        return pltpu.make_async_remote_copy(
            src_ref=src, dst_ref=dst, send_sem=send_sem.at[t, kind], recv_sem=recv_sem.at[t, kind],
            device_id=device, device_id_type=pl.DeviceIdType.MESH,
        )

    def span(t, owner, piece_half):
        return ext.at[t, pl.ds(owner * owned + piece_half * hb, hb)]

    def gather_copy(t):
        return remote(span(t, 1, half), span(t, 1, half), t, GATHER, {"cols": other_half})

    def up_copy(t):
        return remote(span(t, 1, half), span(t, 0, half), t, LOW, {"rows": r + 1})

    def down_copy(t):
        return remote(span(t, 1, half), span(t, 2, half), t, HIGH, {"rows": r - 1})

    def low_forward(t):
        return remote(span(t, 0, half), span(t, 0, half), t, LOW_X, {"cols": other_half})

    def high_forward(t):
        return remote(span(t, 2, half), span(t, 2, half), t, HIGH_X, {"cols": other_half})

    def reduce_copy(t):
        return remote(part.at[pl.ds((1 - half) * hb, hb)], reduced.at[t], t, REDUCE, {"cols": other_half})

    def spread_copy(t):
        place = ext.at[t, pl.ds(owned + half * hb + mode * qb, qb)]
        return remote(share.at[1 - mode], place, t, SPREAD, {"cols": mate})

    def pair_copy(k):
        src = summed.at[k, pl.ds((1 - mode) * qb, qb)]
        return remote(src, pair.at[k], 2 * k + 1, PAIR, {"cols": mate})

    def send_halo(t):
        @pl.when(has_high)
        def _():
            up_copy(t).start()

        @pl.when(has_low)
        def _():
            down_copy(t).start()

        gather_copy(t).start()

    def forward_halo(t):
        @pl.when(has_low)
        def _():
            up_copy(t).wait_recv()
            low_forward(t).start()

        @pl.when(has_high)
        def _():
            down_copy(t).wait_recv()
            high_forward(t).start()

    def finish_halo(t):
        gather_copy(t).wait()

        @pl.when(has_low)
        def _():
            low_forward(t).wait()
            down_copy(t).wait_send()

        @pl.when(has_high)
        def _():
            high_forward(t).wait()
            up_copy(t).wait_send()

    def start_spread(t):
        spread_copy(t).start()
        for b in range(qb):
            ext[t, owned + half * hb + mode * qb + b] = share[mode, b]

    def finish_spread(t):
        spread_copy(t).wait()

    tile_parts = tile_sem.shape[0]
    per = owned // tile_parts

    def tile_local(q):
        rows = pl.ds(q * per, per)
        return pltpu.make_async_copy(tiles_ref.at[rows], own_tiles.at[rows], tile_sem.at[q])

    def tile_remote(q):
        rows = pl.ds(q * per, per)
        return pltpu.make_async_remote_copy(
            src_ref=tiles_ref.at[rows], dst_ref=mate_tiles.at[rows], send_sem=tile_send_sem.at[q],
            recv_sem=tile_recv_sem.at[q], device_id={"cols": mate}, device_id_type=pl.DeviceIdType.MESH,
        )

    slot_remote = pltpu.make_async_remote_copy(
        src_ref=slots_ref, dst_ref=mate_slots, send_sem=slot_sem.at[0], recv_sem=slot_sem.at[1],
        device_id={"cols": mate}, device_id_type=pl.DeviceIdType.MESH,
    )
    slot_remote.start()
    for b in range(qb):
        for h in range(2):
            share[h, b] = start_ref[h * modes : (h + 1) * modes, b * width : (b + 1) * width]
    start_spread(0)
    for q in range(tile_parts):
        tile_local(q).start()
        tile_remote(q).start()
    slot_own = pltpu.make_async_copy(slots_ref, own_index, slot_sem.at[2])
    slot_own.start()
    finish_spread(0)
    send_halo(0)
    slot_remote.wait()
    slot_mate = pltpu.make_async_copy(mate_slots, mate_index, slot_sem.at[3])
    slot_mate.start()
    slot_own.wait()
    slot_mate.wait()

    def split_tiles(source, q, offset):
        def body(i, carry):
            for s in range(slot_dev):
                tile = source[i, s]
                high = tile.astype(BF16)
                lanes = slice((offset + s) * width, (offset + s + 1) * width)
                t_hi[i, :, lanes] = high
                t_lo[i, :, lanes] = (tile - high.astype(F32)).astype(BF16)
            return carry

        lax.fori_loop(q * per, (q + 1) * per, body, 0)

    for q in range(tile_parts):
        tile_local(q).wait()
        split_tiles(own_tiles, q, 0)
    forward_halo(0)
    for q in range(tile_parts):
        tile_remote(q).wait()
        split_tiles(mate_tiles, q, slot_dev)

    weight_rows = lax.broadcasted_iota(jnp.int32, weight.shape, 0)
    weight_lanes = lax.broadcasted_iota(jnp.int32, weight.shape, 1)
    weight[...] = jnp.where(weight_rows == weight_lanes, 1.0, 0.0).astype(F32)
    blocks = 3 * owned
    planes[blocks] = jnp.zeros(planes.shape[1:], BF16)

    def row_product(i):
        picks = [planes[own_index[i, s]] for s in range(slot_dev)]
        picks += [planes[mate_index[i, s]] for s in range(slot_dev)]
        left = jnp.concatenate(picks, axis=1)
        contract = (((1,), (1,)), ((), ()))
        main = lax.dot_general(left, t_hi[i], contract, preferred_element_type=F32)
        rest = lax.dot_general(left[:modes], t_lo[i], contract, preferred_element_type=F32)
        part[i] = main[:modes] + (main[modes:] + rest)

    def apply(t):
        def convert(b, carry):
            value = ext[t, b]
            high = value.astype(BF16)
            planes[b, :modes] = high
            planes[b, modes:] = (value - high.astype(F32)).astype(BF16)
            return carry

        lax.fori_loop(0, blocks, convert, 0, unroll=4)

        def product(i, carry):
            row_product((1 - half) * hb + i)
            return carry

        lax.fori_loop(0, hb, product, 0, unroll=2)
        reduce_copy(t).start()

        def product_own(i, carry):
            row_product(half * hb + i)
            return carry

        lax.fori_loop(0, hb, product_own, 0, unroll=2)
        reduce_copy(t).wait()

    def add_reduced(t, target):
        def body(b, carry):
            ext[target, owned + half * hb + b] = part[half * hb + b] + reduced[t, b]
            return carry

        lax.fori_loop(0, hb, body, 0)

    def gram_round(k, b):
        copy = pltpu.make_async_remote_copy(
            src_ref=gram_send.at[k, b], dst_ref=gram_recv.at[k, b], send_sem=gram_send_sem.at[k, b],
            recv_sem=gram_recv_sem.at[k, b], device_id=gram_partners[b], device_id_type=pl.DeviceIdType.MESH,
        )
        return copy

    rounds = len(gram_partners)

    def sum_round(k, b):
        gram_round(k, b).wait()
        total = gram_send[k, b] + gram_recv[k, b]
        if b + 1 < rounds:
            gram_send[k, b + 1] = total
            gram_round(k, b + 1).start()
        return total

    def sweep(k, carry):
        t = 2 * k
        finish_halo(t)
        apply(t)
        add_reduced(t, t + 1)
        send_halo(t + 1)
        forward_halo(t + 1)
        finish_halo(t + 1)
        apply(t + 1)
        def close(b, carry):
            summed[k, b] = part[half * hb + b] + reduced[t + 1, b]
            return carry

        lax.fori_loop(0, hb, close, 0)
        pair_copy(k).start()
        for b in range(qb):
            share[mode, b] = summed[k, mode * qb + b]
        pair_copy(k).wait()
        for b in range(qb):
            share[1 - mode, b] = pair[k, b]
        raw = jnp.concatenate(
            [jnp.concatenate([share[0, b], share[1, b]], axis=0) for b in range(qb)], axis=1
        )
        mixed = jnp.dot(weight[...], raw, precision=HIGHEST, preferred_element_type=F32)
        for b in range(qb):
            for h in range(2):
                share[h, b] = mixed[h * modes : (h + 1) * modes, b * width : (b + 1) * width]
        gram_send[k, 0] = lax.dot_general(
            mixed, mixed, (((1,), (1,)), ((), ())), precision=HIGHEST, preferred_element_type=F32
        )
        gram_round(k, 0).start()

        more = k < ITERS - 1

        @pl.when(more)
        def _():
            start_spread(t + 2)
            finish_spread(t + 2)
            send_halo(t + 2)

        total = sum_round(k, 0)
        total = sum_round(k, 1)

        @pl.when(more)
        def _():
            forward_halo(t + 2)

        for b in range(2, rounds):
            total = sum_round(k, b)
        weight[...] = inverse_factor(total)
        return carry

    lax.fori_loop(0, ITERS, sweep, 0)
    final = jnp.concatenate(
        [jnp.concatenate([share[0, b], share[1, b]], axis=0) for b in range(qb)], axis=1
    )
    out_ref[...] = jnp.dot(weight[...], final, precision=HIGHEST, preferred_element_type=F32)


def per_device(start_panel, tile_values, tile_column, tile_count):
    n_rows = lax.axis_size("rows")
    n_cols = lax.axis_size("cols")
    owned, slot_dev, width, _ = tile_values.shape
    modes_all, states = start_panel.shape
    modes = modes_all // 2
    hb = owned // 2
    qb = owned // 4
    slot_ids = lax.axis_index("cols") * slot_dev + jnp.arange(slot_dev, dtype=jnp.int32)
    anchor = (lax.axis_index("rows") - 1) * owned
    index = jnp.where(slot_ids[None, :] < tile_count[:, None], tile_column - anchor, 3 * owned)
    index = jnp.pad(index, ((0, 0), (0, 128 - slot_dev)))
    rounds = 2 + int(math.log2(n_rows))
    applies = 2 * ITERS
    vmem = pltpu.VMEM
    dma = pltpu.SemaphoreType.DMA
    anywhere = pl.BlockSpec(memory_space=pl.ANY)
    in_vmem = pl.BlockSpec(memory_space=pltpu.VMEM)
    panel = pl.pallas_call(
        functools.partial(kernel, n_rows),
        out_shape=jax.ShapeDtypeStruct((modes_all, states), F32),
        in_specs=[in_vmem, anywhere, in_vmem],
        out_specs=in_vmem,
        scratch_shapes=[
            vmem((applies, 3 * owned, modes, width), F32),
            vmem((3 * owned + 1, 2 * modes, width), BF16),
            vmem((owned, modes, width), F32),
            vmem((applies, hb, modes, width), F32),
            vmem((ITERS, hb, modes, width), F32),
            vmem((2, qb, modes, width), F32),
            vmem((ITERS, qb, modes, width), F32),
            vmem((owned, slot_dev, width, width), F32),
            vmem((owned, slot_dev, width, width), F32),
            vmem((owned, width, 2 * slot_dev * width), BF16),
            vmem((owned, width, 2 * slot_dev * width), BF16),
            vmem((owned, 128), jnp.int32),
            pltpu.SMEM((owned, 128), jnp.int32),
            pltpu.SMEM((owned, 128), jnp.int32),
            vmem((modes_all, modes_all), F32),
            vmem((ITERS, rounds, modes_all, modes_all), F32),
            vmem((ITERS, rounds, modes_all, modes_all), F32),
            dma((applies, KINDS)),
            dma((applies, KINDS)),
            dma((ITERS, rounds)),
            dma((ITERS, rounds)),
            dma((4,)),
            dma((4,)),
            dma((4,)),
            dma((4,)),
        ],
        compiler_params=pltpu.CompilerParams(
            collective_id=0, has_side_effects=True, vmem_limit_bytes=50 * 1024 * 1024
        ),
        name="subspace_sweeps",
    )(start_panel, tile_values, index)
    scaling = math.sqrt(n_rows * n_cols * states)
    return panel * jnp.float32(scaling)


def solution(mesh):
    in_specs = (
        P(None, ("rows", "cols")),
        P("rows", "cols", None, None),
        P("rows", "cols"),
        P("rows"),
    )
    out_specs = P(None, ("rows", "cols"))
    return jax.shard_map(
        per_device, mesh=mesh, in_specs=in_specs, out_specs=out_specs, check_vma=False
    )
```

```python
import functools
import math

import jax
import jax.numpy as jnp
from jax import lax
from jax.experimental import pallas as pl
from jax.experimental.pallas import tpu as pltpu
from jax.sharding import PartitionSpec as P

ITERS = 3
HIGHEST = lax.Precision.HIGHEST
F32 = jnp.float32
BF16 = jnp.bfloat16

GATHER, LOW, HIGH, LOW_X, HIGH_X, REDUCE, SPREAD, PAIR = range(8)
KINDS = 8
CHUNKS = 4
ROW_BITS = 3


def gram_masks(n_rows):
    stages = [("cols", (1, 2, 3))]
    bits = int(math.log2(n_rows))
    for low in range(0, bits, ROW_BITS):
        count = min(ROW_BITS, bits - low)
        stages.append(("rows", tuple(m << low for m in range(1, 1 << count))))
    return stages


def inverse_factor(gram):
    size = gram.shape[0]
    rows = lax.broadcasted_iota(jnp.int32, (size, size), 0)
    lanes = lax.broadcasted_iota(jnp.int32, (size, size), 1)
    both = jnp.concatenate([gram, jnp.where(rows == lanes, 1.0, 0.0).astype(F32)], axis=1)
    row_ids = lax.broadcasted_iota(jnp.int32, (size, 1), 0)
    scale = jnp.ones((size, 1), F32)
    for j in range(size):
        column = both[:, j : j + 1]
        row = both[j : j + 1, :]
        pivot = both[j : j + 1, j : j + 1]
        factor = jnp.where(row_ids > j, column / pivot, 0.0)
        scale = jnp.where(row_ids == j, lax.rsqrt(pivot), scale)
        both = both - factor * row
    return both[:, size:] * scale


def kernel(
    n_rows, start_ref, tiles_ref, slots_ref, out_ref,
    ext, planes, part, reduced, summed, share, pair, own_tiles, mate_tiles, t_hi, t_lo,
    mate_slots, own_index, mate_index, weight, gram_total, gram_send, gram_recv,
    send_sem, recv_sem, gram_send_sem, gram_recv_sem, tile_sem, tile_send_sem, tile_recv_sem,
    slot_sem,
):
    r = lax.axis_index("rows")
    c = lax.axis_index("cols")
    half = c // 2
    mode = c % 2
    modes = ext.shape[2]
    owned = part.shape[0]
    hb = owned // 2
    qb = owned // 4
    slot_dev = own_tiles.shape[1]
    width = part.shape[2]
    other_half = c + 2 - 4 * half
    mate = c + 1 - 2 * mode
    def flipped(value, mask):
        for b in range(mask.bit_length()):
            if mask >> b & 1:
                step = 1 << b
                value = value + step - 2 * step * ((value // step) % 2)
        return value

    gram_stages = [
        [{axis: flipped(r if axis == "rows" else c, mask)} for mask in masks]
        for axis, masks in gram_masks(n_rows)
    ]
    gram_partners = [partner for stage in gram_stages for partner in stage]

    barrier = pltpu.get_barrier_semaphore()
    for partner in gram_partners:
        pl.semaphore_signal(barrier, inc=1, device_id=partner, device_id_type=pl.DeviceIdType.MESH)
    has_low = r > 0
    has_high = r < n_rows - 1

    @pl.when(has_low)
    def _():
        pl.semaphore_signal(barrier, inc=1, device_id={"rows": r - 1}, device_id_type=pl.DeviceIdType.MESH)

    @pl.when(has_high)
    def _():
        pl.semaphore_signal(barrier, inc=1, device_id={"rows": r + 1}, device_id_type=pl.DeviceIdType.MESH)

    edges = jnp.where(r == 0, 1, 0) + jnp.where(r == n_rows - 1, 1, 0)
    pl.semaphore_wait(barrier, len(gram_partners) + 2 - edges)

    def remote(src, dst, t, kind, device, j=0):
        return pltpu.make_async_remote_copy(
            src_ref=src, dst_ref=dst, send_sem=send_sem.at[t, kind, j], recv_sem=recv_sem.at[t, kind, j],
            device_id=device, device_id_type=pl.DeviceIdType.MESH,
        )

    cb = hb // CHUNKS
    up, down, across = {"rows": r + 1}, {"rows": r - 1}, {"cols": other_half}

    def span(t, owner, piece_half, j):
        return ext.at[t, pl.ds(owner * owned + piece_half * hb + j * cb, cb)]

    def relayed(j):
        return j % 2 == 0

    def gather_copy(t, j):
        return remote(span(t, 1, half, j), span(t, 1, half, j), t, GATHER, across, j)

    def up_copy(t, j):
        return remote(span(t, 1, half, j), span(t, 0, half, j), t, LOW, up, j)

    def down_copy(t, j):
        return remote(span(t, 1, half, j), span(t, 2, half, j), t, HIGH, down, j)

    def relay_up(t, j):
        return remote(span(t, 1, 1 - half, j), span(t, 0, 1 - half, j), t, LOW_X, up, j)

    def relay_down(t, j):
        return remote(span(t, 1, 1 - half, j), span(t, 2, 1 - half, j), t, HIGH_X, down, j)

    def low_forward(t, j):
        return remote(span(t, 0, half, j), span(t, 0, half, j), t, LOW_X, across, j)

    def high_forward(t, j):
        return remote(span(t, 2, half, j), span(t, 2, half, j), t, HIGH_X, across, j)

    def reduce_copy(t, j):
        src = part.at[pl.ds((1 - half) * hb + j * cb, cb)]
        return remote(src, reduced.at[t, pl.ds(j * cb, cb)], t, REDUCE, across, j)

    def pair_copy(k):
        src = summed.at[k, pl.ds((1 - mode) * qb, qb)]
        return remote(src, pair.at[k], 2 * k + 1, PAIR, {"cols": mate})

    def spread_copy(t):
        place = ext.at[t, pl.ds(owned + half * hb + mode * qb, qb)]
        return remote(share.at[1 - mode], place, t, SPREAD, {"cols": mate})

    def pair_copy(k):
        src = summed.at[k, pl.ds((1 - mode) * qb, qb)]
        return remote(src, pair.at[k], 2 * k + 1, PAIR, {"cols": mate})

    def send_chunk(t, j):
        gather_copy(t, j).start()

        @pl.when(has_high)
        def _():
            up_copy(t, j).start()

        @pl.when(has_low)
        def _():
            down_copy(t, j).start()

    def send_halo(t):
        for j in range(CHUNKS):
            send_chunk(t, j)

    def pass_halo(t):
        for j in range(CHUNKS):
            gather_copy(t, j).wait_recv()

            @pl.when(has_high)
            def _():
                if relayed(j):
                    relay_up(t, j).start()
                down_copy(t, j).wait_recv()
                if not relayed(j):
                    high_forward(t, j).start()

            @pl.when(has_low)
            def _():
                if relayed(j):
                    relay_down(t, j).start()
                up_copy(t, j).wait_recv()
                if not relayed(j):
                    low_forward(t, j).start()

    def finish_halo(t):
        for j in range(CHUNKS):
            gather_copy(t, j).wait_send()

            @pl.when(has_low)
            def _():
                down_copy(t, j).wait_send()
                low_forward(t, j).wait_recv()
                (relay_down if relayed(j) else low_forward)(t, j).wait_send()

            @pl.when(has_high)
            def _():
                up_copy(t, j).wait_send()
                high_forward(t, j).wait_recv()
                (relay_up if relayed(j) else high_forward)(t, j).wait_send()

    def start_spread(t):
        spread_copy(t).start()
        for b in range(qb):
            ext[t, owned + half * hb + mode * qb + b] = share[mode, b]

    def finish_spread(t):
        spread_copy(t).wait()

    tile_parts = tile_sem.shape[0]
    per = owned // tile_parts

    def tile_local(q):
        rows = pl.ds(q * per, per)
        return pltpu.make_async_copy(tiles_ref.at[rows], own_tiles.at[rows], tile_sem.at[q])

    def tile_remote(q):
        rows = pl.ds(q * per, per)
        return pltpu.make_async_remote_copy(
            src_ref=tiles_ref.at[rows], dst_ref=mate_tiles.at[rows], send_sem=tile_send_sem.at[q],
            recv_sem=tile_recv_sem.at[q], device_id={"cols": mate}, device_id_type=pl.DeviceIdType.MESH,
        )

    slot_remote = pltpu.make_async_remote_copy(
        src_ref=slots_ref, dst_ref=mate_slots, send_sem=slot_sem.at[0], recv_sem=slot_sem.at[1],
        device_id={"cols": mate}, device_id_type=pl.DeviceIdType.MESH,
    )
    slot_remote.start()
    for b in range(qb):
        for h in range(2):
            share[h, b] = start_ref[h * modes : (h + 1) * modes, b * width : (b + 1) * width]
    start_spread(0)
    for q in range(tile_parts):
        tile_local(q).start()
        tile_remote(q).start()
    slot_own = pltpu.make_async_copy(slots_ref, own_index, slot_sem.at[2])
    slot_own.start()
    finish_spread(0)
    send_halo(0)
    slot_remote.wait()
    slot_mate = pltpu.make_async_copy(mate_slots, mate_index, slot_sem.at[3])
    slot_mate.start()
    slot_own.wait()
    slot_mate.wait()

    def split_tiles(source, q, offset):
        def body(i, carry):
            for s in range(slot_dev):
                tile = source[i, s]
                high = tile.astype(BF16)
                lanes = slice((offset + s) * width, (offset + s + 1) * width)
                t_hi[i, :, lanes] = high
                t_lo[i, :, lanes] = (tile - high.astype(F32)).astype(BF16)
            return carry

        lax.fori_loop(q * per, (q + 1) * per, body, 0)

    for q in range(tile_parts):
        tile_local(q).wait()
        split_tiles(own_tiles, q, 0)
    for q in range(tile_parts):
        tile_remote(q).wait()
        split_tiles(mate_tiles, q, slot_dev)

    weight_rows = lax.broadcasted_iota(jnp.int32, weight.shape, 0)
    weight_lanes = lax.broadcasted_iota(jnp.int32, weight.shape, 1)
    weight[...] = jnp.where(weight_rows == weight_lanes, 1.0, 0.0).astype(F32)
    blocks = 3 * owned
    planes[blocks] = jnp.zeros(planes.shape[1:], BF16)

    def row_product(i):
        picks = [planes[own_index[i, s]] for s in range(slot_dev)]
        picks += [planes[mate_index[i, s]] for s in range(slot_dev)]
        left = jnp.concatenate(picks, axis=1)
        contract = (((1,), (1,)), ((), ()))
        main = lax.dot_general(left, t_hi[i], contract, preferred_element_type=F32)
        rest = lax.dot_general(left[:modes], t_lo[i], contract, preferred_element_type=F32)
        part[i] = main[:modes] + (main[modes:] + rest)

    def apply(t):
        def convert(b, carry):
            value = ext[t, b]
            high = value.astype(BF16)
            planes[b, :modes] = high
            planes[b, modes:] = (value - high.astype(F32)).astype(BF16)
            return carry

        lax.fori_loop(0, blocks, convert, 0, unroll=4)

        for first in (1 - half, half):
            for j in range(CHUNKS):
                def product(i, carry):
                    row_product(first * hb + j * cb + i)
                    return carry

                lax.fori_loop(0, cb, product, 0, unroll=True)
                if first is not half:
                    reduce_copy(t, j).start()

    def reduce_chunk(t, j):
        reduce_copy(t, j).wait_recv()
        return [(j * cb + b, part[half * hb + j * cb + b] + reduced[t, j * cb + b]) for b in range(cb)]

    def finish_reduce(t):
        for j in range(CHUNKS):
            reduce_copy(t, j).wait_send()

    offsets = [0]
    for stage in gram_stages:
        offsets.append(offsets[-1] + len(stage))

    def gram_copy(k, stage, p):
        slot = offsets[stage] + p
        return pltpu.make_async_remote_copy(
            src_ref=gram_send.at[k, stage], dst_ref=gram_recv.at[k, slot], send_sem=gram_send_sem.at[k, slot],
            recv_sem=gram_recv_sem.at[k, slot], device_id=gram_stages[stage][p],
            device_id_type=pl.DeviceIdType.MESH,
        )

    def start_stage(k, stage, value):
        gram_send[k, stage] = value
        for p in range(len(gram_stages[stage])):
            gram_copy(k, stage, p).start()

    def end_stage(k, stage):
        terms = [gram_send[k, stage]]
        for p in range(len(gram_stages[stage])):
            gram_copy(k, stage, p).wait()
            terms.append(gram_recv[k, offsets[stage] + p])
        while len(terms) > 1:
            terms = [terms[p] + terms[p + 1] for p in range(0, len(terms), 2)]
        if stage + 1 < len(gram_stages):
            start_stage(k, stage + 1, terms[0])
        else:
            gram_total[...] = terms[0]

    def factor(k):
        for stage in range(2, len(gram_stages)):
            end_stage(k, stage)
        weight[...] = inverse_factor(gram_total[...])

    def sweep(k, carry):
        t = 2 * k
        later = k > 0
        pass_halo(t)

        @pl.when(later)
        def _():
            end_stage(k - 1, 0)

        finish_halo(t)
        apply(t)

        @pl.when(later)
        def _():
            end_stage(k - 1, 1)

        for j in range(CHUNKS):
            for b, value in reduce_chunk(t, j):
                ext[t + 1, owned + half * hb + b] = value
            send_chunk(t + 1, j)
        finish_reduce(t)
        pass_halo(t + 1)

        @pl.when(later)
        def _():
            factor(k - 1)

        finish_halo(t + 1)
        apply(t + 1)
        for j in range(CHUNKS):
            for b, value in reduce_chunk(t + 1, j):
                summed[k, b] = value
        finish_reduce(t + 1)
        pair_copy(k).start()
        for b in range(qb):
            share[mode, b] = summed[k, mode * qb + b]
        pair_copy(k).wait()
        for b in range(qb):
            share[1 - mode, b] = pair[k, b]
        raw = jnp.concatenate(
            [jnp.concatenate([share[0, b], share[1, b]], axis=0) for b in range(qb)], axis=1
        )
        mixed = jnp.dot(weight[...], raw, precision=HIGHEST, preferred_element_type=F32)
        for b in range(qb):
            for h in range(2):
                share[h, b] = mixed[h * modes : (h + 1) * modes, b * width : (b + 1) * width]
        gram = lax.dot_general(
            mixed, mixed, (((1,), (1,)), ((), ())), precision=HIGHEST, preferred_element_type=F32
        )
        start_stage(k, 0, gram)

        @pl.when(k < ITERS - 1)
        def _():
            start_spread(t + 2)
            finish_spread(t + 2)
            send_halo(t + 2)

        return carry

    lax.fori_loop(0, ITERS, sweep, 0)
    end_stage(ITERS - 1, 0)
    end_stage(ITERS - 1, 1)
    factor(ITERS - 1)
    final = jnp.concatenate(
        [jnp.concatenate([share[0, b], share[1, b]], axis=0) for b in range(qb)], axis=1
    )
    out_ref[...] = jnp.dot(weight[...], final, precision=HIGHEST, preferred_element_type=F32)


def per_device(start_panel, tile_values, tile_column, tile_count):
    n_rows = lax.axis_size("rows")
    n_cols = lax.axis_size("cols")
    owned, slot_dev, width, _ = tile_values.shape
    modes_all, states = start_panel.shape
    modes = modes_all // 2
    hb = owned // 2
    qb = owned // 4
    slot_ids = lax.axis_index("cols") * slot_dev + jnp.arange(slot_dev, dtype=jnp.int32)
    anchor = (lax.axis_index("rows") - 1) * owned
    index = jnp.where(slot_ids[None, :] < tile_count[:, None], tile_column - anchor, 3 * owned)
    index = jnp.pad(index, ((0, 0), (0, 128 - slot_dev)))
    stages = gram_masks(n_rows)
    peers = sum(len(masks) for _, masks in stages)
    applies = 2 * ITERS
    vmem = pltpu.VMEM
    dma = pltpu.SemaphoreType.DMA
    anywhere = pl.BlockSpec(memory_space=pl.ANY)
    in_vmem = pl.BlockSpec(memory_space=pltpu.VMEM)
    panel = pl.pallas_call(
        functools.partial(kernel, n_rows),
        out_shape=jax.ShapeDtypeStruct((modes_all, states), F32),
        in_specs=[in_vmem, anywhere, in_vmem],
        out_specs=in_vmem,
        scratch_shapes=[
            vmem((applies, 3 * owned, modes, width), F32),
            vmem((3 * owned + 1, 2 * modes, width), BF16),
            vmem((owned, modes, width), F32),
            vmem((applies, hb, modes, width), F32),
            vmem((ITERS, hb, modes, width), F32),
            vmem((2, qb, modes, width), F32),
            vmem((ITERS, qb, modes, width), F32),
            vmem((owned, slot_dev, width, width), F32),
            vmem((owned, slot_dev, width, width), F32),
            vmem((owned, width, 2 * slot_dev * width), BF16),
            vmem((owned, width, 2 * slot_dev * width), BF16),
            vmem((owned, 128), jnp.int32),
            pltpu.SMEM((owned, 128), jnp.int32),
            pltpu.SMEM((owned, 128), jnp.int32),
            vmem((modes_all, modes_all), F32),
            vmem((modes_all, modes_all), F32),
            vmem((ITERS, len(stages), modes_all, modes_all), F32),
            vmem((ITERS, peers, modes_all, modes_all), F32),
            dma((applies, KINDS, CHUNKS)),
            dma((applies, KINDS, CHUNKS)),
            dma((ITERS, peers)),
            dma((ITERS, peers)),
            dma((4,)),
            dma((4,)),
            dma((4,)),
            dma((4,)),
        ],
        compiler_params=pltpu.CompilerParams(
            collective_id=0, has_side_effects=True, vmem_limit_bytes=50 * 1024 * 1024
        ),
        name="subspace_sweeps",
    )(start_panel, tile_values, index)
    scaling = math.sqrt(n_rows * n_cols * states)
    return panel * jnp.float32(scaling)


def solution(mesh):
    in_specs = (
        P(None, ("rows", "cols")),
        P("rows", "cols", None, None),
        P("rows", "cols"),
        P("rows"),
    )
    out_specs = P(None, ("rows", "cols"))
    return jax.shard_map(
        per_device, mesh=mesh, in_specs=in_specs, out_specs=out_specs, check_vma=False
    )
```

```python
import functools
import math

import jax
import jax.numpy as jnp
from jax import lax
from jax.experimental import pallas as pl
from jax.experimental.pallas import tpu as pltpu
from jax.sharding import PartitionSpec as P

ITERS = 3
HIGHEST = lax.Precision.HIGHEST
F32 = jnp.float32
BF16 = jnp.bfloat16

GATHER, LOW, HIGH, LOW_X, HIGH_X, REDUCE, SPREAD, PAIR = range(8)
KINDS = 8
CHUNKS = 4
ROW_BITS = 3


def gram_masks(n_rows):
    stages = [("cols", (1, 2, 3))]
    bits = int(math.log2(n_rows))
    for low in range(0, bits, ROW_BITS):
        count = min(ROW_BITS, bits - low)
        stages.append(("rows", tuple(m << low for m in range(1, 1 << count))))
    return stages


def inverse_factor(gram):
    size = gram.shape[0]
    rows = lax.broadcasted_iota(jnp.int32, (size, size), 0)
    lanes = lax.broadcasted_iota(jnp.int32, (size, size), 1)
    both = jnp.concatenate([gram, jnp.where(rows == lanes, 1.0, 0.0).astype(F32)], axis=1)
    row_ids = lax.broadcasted_iota(jnp.int32, (size, 1), 0)
    scale = jnp.ones((size, 1), F32)
    for j in range(size):
        column = both[:, j : j + 1]
        row = both[j : j + 1, :]
        pivot = both[j : j + 1, j : j + 1]
        factor = jnp.where(row_ids > j, column, 0.0) * (1.0 / pivot)
        scale = jnp.where(row_ids == j, lax.rsqrt(pivot), scale)
        both = both - factor * row
    return both[:, size:] * scale


def kernel(
    n_rows, start_ref, tiles_ref, slots_ref, out_ref,
    ext, planes, part, reduced, summed, share, pair, own_tiles, mate_tiles, t_hi, t_lo,
    mate_slots, own_index, mate_index, weight, gram_total, gram_send, gram_recv,
    send_sem, recv_sem, gram_send_sem, gram_recv_sem, tile_sem, tile_send_sem, tile_recv_sem,
    slot_sem,
):
    r = lax.axis_index("rows")
    c = lax.axis_index("cols")
    half = c // 2
    mode = c % 2
    modes = ext.shape[2]
    owned = part.shape[0]
    hb = owned // 2
    qb = owned // 4
    slot_dev = own_tiles.shape[1]
    width = part.shape[2]
    other_half = c + 2 - 4 * half
    mate = c + 1 - 2 * mode
    def flipped(value, mask):
        for b in range(mask.bit_length()):
            if mask >> b & 1:
                step = 1 << b
                value = value + step - 2 * step * ((value // step) % 2)
        return value

    gram_stages = [
        [{axis: flipped(r if axis == "rows" else c, mask)} for mask in masks]
        for axis, masks in gram_masks(n_rows)
    ]
    gram_partners = [partner for stage in gram_stages for partner in stage]

    barrier = pltpu.get_barrier_semaphore()
    for partner in gram_partners:
        pl.semaphore_signal(barrier, inc=1, device_id=partner, device_id_type=pl.DeviceIdType.MESH)
    has_low = r > 0
    has_high = r < n_rows - 1

    @pl.when(has_low)
    def _():
        pl.semaphore_signal(barrier, inc=1, device_id={"rows": r - 1}, device_id_type=pl.DeviceIdType.MESH)

    @pl.when(has_high)
    def _():
        pl.semaphore_signal(barrier, inc=1, device_id={"rows": r + 1}, device_id_type=pl.DeviceIdType.MESH)

    edges = jnp.where(r == 0, 1, 0) + jnp.where(r == n_rows - 1, 1, 0)
    pl.semaphore_wait(barrier, len(gram_partners) + 2 - edges)

    def remote(src, dst, t, kind, device, j=0):
        return pltpu.make_async_remote_copy(
            src_ref=src, dst_ref=dst, send_sem=send_sem.at[t, kind, j], recv_sem=recv_sem.at[t, kind, j],
            device_id=device, device_id_type=pl.DeviceIdType.MESH,
        )

    cb = hb // CHUNKS
    up, down, across = {"rows": r + 1}, {"rows": r - 1}, {"cols": other_half}

    def span(t, owner, piece_half, j):
        return ext.at[t, pl.ds(owner * owned + piece_half * hb + j * cb, cb)]

    def relayed(j):
        return False

    def gather_copy(t, j):
        return remote(span(t, 1, half, j), span(t, 1, half, j), t, GATHER, across, j)

    def up_copy(t, j):
        return remote(span(t, 1, half, j), span(t, 0, half, j), t, LOW, up, j)

    def down_copy(t, j):
        return remote(span(t, 1, half, j), span(t, 2, half, j), t, HIGH, down, j)

    def relay_up(t, j):
        return remote(span(t, 1, 1 - half, j), span(t, 0, 1 - half, j), t, LOW_X, up, j)

    def relay_down(t, j):
        return remote(span(t, 1, 1 - half, j), span(t, 2, 1 - half, j), t, HIGH_X, down, j)

    def low_forward(t, j):
        return remote(span(t, 0, half, j), span(t, 0, half, j), t, LOW_X, across, j)

    def high_forward(t, j):
        return remote(span(t, 2, half, j), span(t, 2, half, j), t, HIGH_X, across, j)

    def reduce_copy(t, j):
        src = part.at[pl.ds((1 - half) * hb + j * cb, cb)]
        return remote(src, reduced.at[t, pl.ds(j * cb, cb)], t, REDUCE, across, j)

    def pair_copy(k):
        src = summed.at[k, pl.ds((1 - mode) * qb, qb)]
        return remote(src, pair.at[k], 2 * k + 1, PAIR, {"cols": mate})

    def spread_copy(t):
        place = ext.at[t, pl.ds(owned + half * hb + mode * qb, qb)]
        return remote(share.at[1 - mode], place, t, SPREAD, {"cols": mate})

    def pair_copy(k):
        src = summed.at[k, pl.ds((1 - mode) * qb, qb)]
        return remote(src, pair.at[k], 2 * k + 1, PAIR, {"cols": mate})

    def send_chunk(t, j):
        gather_copy(t, j).start()

        @pl.when(has_high)
        def _():
            up_copy(t, j).start()

        @pl.when(has_low)
        def _():
            down_copy(t, j).start()

    def send_halo(t):
        for j in range(CHUNKS):
            send_chunk(t, j)

    def pass_halo(t):
        for j in range(CHUNKS):
            if relayed(j):
                gather_copy(t, j).wait_recv()

            @pl.when(has_high)
            def _():
                if relayed(j):
                    relay_up(t, j).start()
                down_copy(t, j).wait_recv()
                if not relayed(j):
                    high_forward(t, j).start()

            @pl.when(has_low)
            def _():
                if relayed(j):
                    relay_down(t, j).start()
                up_copy(t, j).wait_recv()
                if not relayed(j):
                    low_forward(t, j).start()

    def finish_halo(t):
        for j in range(CHUNKS):
            gather_copy(t, j).wait_send()
            if not relayed(j):
                gather_copy(t, j).wait_recv()

            @pl.when(has_low)
            def _():
                down_copy(t, j).wait_send()
                low_forward(t, j).wait_recv()
                (relay_down if relayed(j) else low_forward)(t, j).wait_send()

            @pl.when(has_high)
            def _():
                up_copy(t, j).wait_send()
                high_forward(t, j).wait_recv()
                (relay_up if relayed(j) else high_forward)(t, j).wait_send()

    def start_spread(t):
        spread_copy(t).start()
        for b in range(qb):
            ext[t, owned + half * hb + mode * qb + b] = share[mode, b]

    def finish_spread(t):
        spread_copy(t).wait()

    tile_parts = tile_sem.shape[0]
    per = owned // tile_parts

    def tile_local(q):
        rows = pl.ds(q * per, per)
        return pltpu.make_async_copy(tiles_ref.at[rows], own_tiles.at[rows], tile_sem.at[q])

    def tile_remote(q):
        rows = pl.ds(q * per, per)
        return pltpu.make_async_remote_copy(
            src_ref=tiles_ref.at[rows], dst_ref=mate_tiles.at[rows], send_sem=tile_send_sem.at[q],
            recv_sem=tile_recv_sem.at[q], device_id={"cols": mate}, device_id_type=pl.DeviceIdType.MESH,
        )

    slot_remote = pltpu.make_async_remote_copy(
        src_ref=slots_ref, dst_ref=mate_slots, send_sem=slot_sem.at[0], recv_sem=slot_sem.at[1],
        device_id={"cols": mate}, device_id_type=pl.DeviceIdType.MESH,
    )
    slot_remote.start()
    for b in range(qb):
        for h in range(2):
            share[h, b] = start_ref[h * modes : (h + 1) * modes, b * width : (b + 1) * width]
    start_spread(0)
    for q in range(tile_parts):
        tile_local(q).start()
        tile_remote(q).start()
    slot_own = pltpu.make_async_copy(slots_ref, own_index, slot_sem.at[2])
    slot_own.start()
    finish_spread(0)
    send_halo(0)
    slot_remote.wait()
    slot_mate = pltpu.make_async_copy(mate_slots, mate_index, slot_sem.at[3])
    slot_mate.start()
    slot_own.wait()
    slot_mate.wait()

    def split_tiles(source, q, offset):
        def body(i, carry):
            for s in range(slot_dev):
                tile = source[i, s]
                high = tile.astype(BF16)
                lanes = slice((offset + s) * width, (offset + s + 1) * width)
                t_hi[i, :, lanes] = high
                t_lo[i, :, lanes] = (tile - high.astype(F32)).astype(BF16)
            return carry

        lax.fori_loop(q * per, (q + 1) * per, body, 0)

    for q in range(tile_parts):
        tile_local(q).wait()
        split_tiles(own_tiles, q, 0)
    pass_halo(0)
    for q in range(tile_parts):
        tile_remote(q).wait()
        split_tiles(mate_tiles, q, slot_dev)

    weight_rows = lax.broadcasted_iota(jnp.int32, weight.shape, 0)
    weight_lanes = lax.broadcasted_iota(jnp.int32, weight.shape, 1)
    weight[...] = jnp.where(weight_rows == weight_lanes, 1.0, 0.0).astype(F32)
    blocks = 3 * owned
    planes[blocks] = jnp.zeros(planes.shape[1:], BF16)

    def row_product(i):
        picks = [planes[own_index[i, s]] for s in range(slot_dev)]
        picks += [planes[mate_index[i, s]] for s in range(slot_dev)]
        left = jnp.concatenate(picks, axis=1)
        contract = (((1,), (1,)), ((), ()))
        main = lax.dot_general(left, t_hi[i], contract, preferred_element_type=F32)
        rest = lax.dot_general(left[:modes], t_lo[i], contract, preferred_element_type=F32)
        part[i] = main[:modes] + (main[modes:] + rest)

    def apply(t):
        def convert(b, carry):
            value = ext[t, b]
            high = value.astype(BF16)
            planes[b, :modes] = high
            planes[b, modes:] = (value - high.astype(F32)).astype(BF16)
            return carry

        lax.fori_loop(0, blocks, convert, 0, unroll=4)

        for first in (1 - half, half):
            for j in range(CHUNKS):
                def product(i, carry):
                    row_product(first * hb + j * cb + i)
                    return carry

                lax.fori_loop(0, cb, product, 0, unroll=True)
                if first is not half:
                    reduce_copy(t, j).start()

    def reduce_chunk(t, j):
        reduce_copy(t, j).wait_recv()
        return [(j * cb + b, part[half * hb + j * cb + b] + reduced[t, j * cb + b]) for b in range(cb)]

    def finish_reduce(t):
        for j in range(CHUNKS):
            reduce_copy(t, j).wait_send()

    offsets = [0]
    for stage in gram_stages:
        offsets.append(offsets[-1] + len(stage))

    def gram_copy(k, stage, p):
        slot = offsets[stage] + p
        return pltpu.make_async_remote_copy(
            src_ref=gram_send.at[k, stage], dst_ref=gram_recv.at[k, slot], send_sem=gram_send_sem.at[k, slot],
            recv_sem=gram_recv_sem.at[k, slot], device_id=gram_stages[stage][p],
            device_id_type=pl.DeviceIdType.MESH,
        )

    def start_stage(k, stage, value):
        gram_send[k, stage] = value
        for p in range(len(gram_stages[stage])):
            gram_copy(k, stage, p).start()

    def end_stage(k, stage):
        terms = [gram_send[k, stage]]
        for p in range(len(gram_stages[stage])):
            gram_copy(k, stage, p).wait()
            terms.append(gram_recv[k, offsets[stage] + p])
        while len(terms) > 1:
            terms = [terms[p] + terms[p + 1] for p in range(0, len(terms), 2)]
        if stage + 1 < len(gram_stages):
            start_stage(k, stage + 1, terms[0])
        else:
            gram_total[...] = terms[0]

    def factor(k):
        for stage in range(2, len(gram_stages)):
            end_stage(k, stage)
        weight[...] = inverse_factor(gram_total[...])

    def sweep(k, carry):
        t = 2 * k
        later = k > 0

        @pl.when(later)
        def _():
            end_stage(k - 1, 0)

        finish_halo(t)
        apply(t)

        @pl.when(later)
        def _():
            end_stage(k - 1, 1)

        for j in range(CHUNKS):
            for b, value in reduce_chunk(t, j):
                ext[t + 1, owned + half * hb + b] = value
            send_chunk(t + 1, j)
        finish_reduce(t)
        pass_halo(t + 1)

        @pl.when(later)
        def _():
            factor(k - 1)

        finish_halo(t + 1)
        apply(t + 1)
        for j in range(CHUNKS):
            for b, value in reduce_chunk(t + 1, j):
                summed[k, b] = value
        finish_reduce(t + 1)
        pair_copy(k).start()
        for b in range(qb):
            share[mode, b] = summed[k, mode * qb + b]
        pair_copy(k).wait()
        for b in range(qb):
            share[1 - mode, b] = pair[k, b]
        raw = jnp.concatenate(
            [jnp.concatenate([share[0, b], share[1, b]], axis=0) for b in range(qb)], axis=1
        )
        mixed = jnp.dot(weight[...], raw, precision=HIGHEST, preferred_element_type=F32)
        for b in range(qb):
            for h in range(2):
                share[h, b] = mixed[h * modes : (h + 1) * modes, b * width : (b + 1) * width]
        more = k < ITERS - 1

        @pl.when(more)
        def _():
            start_spread(t + 2)

        gram = lax.dot_general(
            mixed, mixed, (((1,), (1,)), ((), ())), precision=HIGHEST, preferred_element_type=F32
        )
        start_stage(k, 0, gram)

        @pl.when(more)
        def _():
            finish_spread(t + 2)
            send_halo(t + 2)
            pass_halo(t + 2)

        return carry

    lax.fori_loop(0, ITERS, sweep, 0)
    end_stage(ITERS - 1, 0)
    end_stage(ITERS - 1, 1)
    factor(ITERS - 1)
    final = jnp.concatenate(
        [jnp.concatenate([share[0, b], share[1, b]], axis=0) for b in range(qb)], axis=1
    )
    out_ref[...] = jnp.dot(weight[...], final, precision=HIGHEST, preferred_element_type=F32)


def per_device(start_panel, tile_values, tile_column, tile_count):
    n_rows = lax.axis_size("rows")
    n_cols = lax.axis_size("cols")
    owned, slot_dev, width, _ = tile_values.shape
    modes_all, states = start_panel.shape
    modes = modes_all // 2
    hb = owned // 2
    qb = owned // 4
    slot_ids = lax.axis_index("cols") * slot_dev + jnp.arange(slot_dev, dtype=jnp.int32)
    anchor = (lax.axis_index("rows") - 1) * owned
    index = jnp.where(slot_ids[None, :] < tile_count[:, None], tile_column - anchor, 3 * owned)
    index = jnp.pad(index, ((0, 0), (0, 128 - slot_dev)))
    stages = gram_masks(n_rows)
    peers = sum(len(masks) for _, masks in stages)
    applies = 2 * ITERS
    vmem = pltpu.VMEM
    dma = pltpu.SemaphoreType.DMA
    anywhere = pl.BlockSpec(memory_space=pl.ANY)
    in_vmem = pl.BlockSpec(memory_space=pltpu.VMEM)
    panel = pl.pallas_call(
        functools.partial(kernel, n_rows),
        out_shape=jax.ShapeDtypeStruct((modes_all, states), F32),
        in_specs=[in_vmem, anywhere, in_vmem],
        out_specs=in_vmem,
        scratch_shapes=[
            vmem((applies, 3 * owned, modes, width), F32),
            vmem((3 * owned + 1, 2 * modes, width), BF16),
            vmem((owned, modes, width), F32),
            vmem((applies, hb, modes, width), F32),
            vmem((ITERS, hb, modes, width), F32),
            vmem((2, qb, modes, width), F32),
            vmem((ITERS, qb, modes, width), F32),
            vmem((owned, slot_dev, width, width), F32),
            vmem((owned, slot_dev, width, width), F32),
            vmem((owned, width, 2 * slot_dev * width), BF16),
            vmem((owned, width, 2 * slot_dev * width), BF16),
            vmem((owned, 128), jnp.int32),
            pltpu.SMEM((owned, 128), jnp.int32),
            pltpu.SMEM((owned, 128), jnp.int32),
            vmem((modes_all, modes_all), F32),
            vmem((modes_all, modes_all), F32),
            vmem((ITERS, len(stages), modes_all, modes_all), F32),
            vmem((ITERS, peers, modes_all, modes_all), F32),
            dma((applies, KINDS, CHUNKS)),
            dma((applies, KINDS, CHUNKS)),
            dma((ITERS, peers)),
            dma((ITERS, peers)),
            dma((4,)),
            dma((4,)),
            dma((4,)),
            dma((4,)),
        ],
        compiler_params=pltpu.CompilerParams(
            collective_id=0, has_side_effects=True, vmem_limit_bytes=50 * 1024 * 1024
        ),
        name="subspace_sweeps",
    )(start_panel, tile_values, index)
    scaling = math.sqrt(n_rows * n_cols * states)
    return panel * jnp.float32(scaling)


def solution(mesh):
    in_specs = (
        P(None, ("rows", "cols")),
        P("rows", "cols", None, None),
        P("rows", "cols"),
        P("rows"),
    )
    out_specs = P(None, ("rows", "cols"))
    return jax.shard_map(
        per_device, mesh=mesh, in_specs=in_specs, out_specs=out_specs, check_vma=False
    )
```
